32 devices in a mesh: dp: 8 (over z, y), fsdp: 4 (over x, core).
Axes of the slice: x: 2, y: 2, z: 4, core: 2. Of those that a mesh axis runs over, the one named last changes fastest.
Arguments:
- hidden_in: bfloat16 [32, 512, 768], P(('dp', 'fsdp')), may hold values from -6 to 6
- segment_ids: int32 [32, 512], P(('dp', 'fsdp')), may hold values from 0 to 2, never falling along the last dimension, each value on 1 to 256 neighbouring positions
- norm_gain: bfloat16 [768], P(('dp', 'fsdp')), may hold values from 0.5 to 1.5
- in_weight: bfloat16 [768, 3352], P(('dp', 'fsdp')), may hold values from -0.21875 to 0.21875
- conv_weight: bfloat16 [4, 1792], P(None, ('dp', 'fsdp')), may hold values from -3 to 3
- conv_bias: bfloat16 [1792], P(('dp', 'fsdp')), may hold values from -0.5 to 0.5
- gate_gain: bfloat16 [1536], P(('dp', 'fsdp')), may hold values from 0.5 to 1.5
- out_weight: bfloat16 [1536, 768], P(('dp', 'fsdp')), may hold values from -0.15625 to 0.15625
- step_bias: float32 [24], replicated, may hold values from -6.9 to -2.3
- decay_log: float32 [24], replicated, may hold values from 0 to 2.77
- skip_weight: float32 [24], replicated, may hold values from 0.5 to 1.5
- cotangent: bfloat16 [32, 512, 768], P(('dp', 'fsdp')), may hold values from -6 to 6
Outputs:
- layer_out: bfloat16 [32, 512, 768], P(('dp', 'fsdp'))
- hidden_grad: bfloat16 [32, 512, 768], P(('dp', 'fsdp'))
- grad_norm_gain: float32 [768], P(('dp', 'fsdp'))
- grad_in_weight: float32 [768, 3352], P(('dp', 'fsdp'))
- grad_conv_weight: float32 [4, 1792], P(None, ('dp', 'fsdp'))
- grad_conv_bias: float32 [1792], P(('dp', 'fsdp'))
- grad_gate_gain: float32 [1536], P(('dp', 'fsdp'))
- grad_out_weight: float32 [1536, 768], P(('dp', 'fsdp'))
- grad_step_bias: float32 [24], replicated
- grad_decay_log: float32 [24], replicated
- grad_skip_weight: float32 [24], replicated
The draws below stay inside these ranges and needn't reach their ends.
Inputs may be any that keep to these rules, and one draw needn't show every extreme that they name: `segment_ids`: segment numbers never fall along a sequence; each sequence holds documents 0, 1 and 2, none longer than half of 512 tokens, and one exactly that long.
All inputs are finite; a program needn't handle non-finite values.
Results may differ from the reference program's by a relative error of at most 0.0087.
Values may be sent and summed in bfloat16 or wider, within the bound.
No kernel may reach another device: no remote copies, remote signals or barrier semaphores. Data moves between devices by JAX's collectives and lax.ppermute only.
A program may use at most 256 MiB of HBM per device.

```python
import math
import jax
import jax.numpy as jnp
import numpy as np
from jax import lax

D = 768
E = 1536
H = 24
CONV = 4
BLOCK = 256
LEN = 512
SEQS = 32
XBC = 1792
PROJ = 3352


def with_spikes(values, rng, source, target, blocks, factor):
    def block_of(position):
        return (jnp.arange(values.shape[position]) // (values.shape[position] // blocks)).reshape((-1,) + (1,) * (values.ndim - 1 - position))

    near = jax.random.permutation(rng, blocks)[block_of(target)]
    far = (block_of(target) + blocks // 2) % blocks
    return jnp.where((block_of(source) == near) | (block_of(source) == far), factor * values, values)


def level_of(key, shape, shards, low, top_value):
    def one(axis_at, shards_of):
        heights = jax.random.uniform(jax.random.fold_in(jax.random.fold_in(key, 6), axis_at), (shards_of,), jnp.float32, low / len(shards), top_value / len(shards))
        return jnp.repeat(jnp.exp(heights), shape[axis_at] // shards_of).reshape((-1,) + (1,) * (len(shape) - axis_at - 1))

    level = one(*shards[0])
    for cut in shards[1:]:
        level = level * one(*cut)
    return level


def profile(number_of, total, bound, lean):
    loads = [(1 << 20) // math.isqrt(rank ** lean) + 1 for rank in range(2, number_of + 1)]
    rest, holding = total - bound - (number_of - 1), [1] * (number_of - 1)
    while rest > 0:
        free = [i for i in range(number_of - 1) if holding[i] < bound]
        whole, remaining = sum([loads[i] for i in free]), rest
        for i in free:
            addition = min(bound - holding[i], max(1, remaining * loads[i] // whole), rest)
            holding[i] = holding[i] + addition
            rest = rest - addition
    return np.array([bound] + holding)


def uneven(stream_key, amount, total, limit, slope):
    if amount == 2:
        one = jax.random.randint(stream_key, (), max(1, total - limit), min(limit, total - 1) + 1)
        return jnp.stack([one, total - one])
    sizes = jnp.asarray(profile(amount, total, limit, slope), jnp.int32)
    pairs = (amount - 1) // 2
    source_of, sink = sizes[1:1 + 2 * pairs:2], sizes[2:2 + 2 * pairs:2]
    margin = jnp.minimum(source_of - 1, limit - sink)
    moved = jax.random.randint(jax.random.fold_in(stream_key, 1), (pairs,), 0, 1 << 20) % (margin + 1)
    sizes = sizes.at[1:1 + 2 * pairs:2].set(source_of - moved).at[2:2 + 2 * pairs:2].set(sink + moved)
    return sizes[jax.random.permutation(jax.random.fold_in(stream_key, 2), amount)]


def gaussian(rng, shape, deviation, limit, cuts=(), kind=jnp.bfloat16):
    level = level_of(rng, shape, cuts, -0.22, 0.18) if cuts else 1.0
    result = jax.random.normal(rng, shape, jnp.float32) * deviation * level
    return jnp.minimum(jnp.maximum(result, -limit), limit).astype(kind)


def heavy_noise(stream_key, shape, spread, reach, split, heavy, held_as=jnp.bfloat16):
    array = spread * jax.random.normal(stream_key, shape, jnp.float32)
    if split:
        array = array * level_of(stream_key, shape, split, -0.22, 0.18)
    return jnp.clip(with_spikes(array, jax.random.fold_in(stream_key, 3), *heavy), -reach, reach).astype(held_as)


def setup_inputs(seed: int = 0) -> dict:
    arg_keys = jax.random.split(jax.random.key(seed), 13)
    hidden_in = heavy_noise(arg_keys[0], (SEQS, LEN, D), 1.0, 6.0, ((0, 32),), (0, 2, 32, 2.75))
    segment_ids = jax.vmap(lambda own: jnp.searchsorted(jnp.cumsum(uneven(own, 3, LEN, LEN // 2, 0)), jnp.arange(LEN), side="right"))(jax.random.split(arg_keys[1], SEQS)).reshape((SEQS, LEN)).astype(jnp.int32)
    norm_gain = jnp.clip(1.0 + 0.1 * jax.random.normal(arg_keys[2], (D,), jnp.float32), 0.5, 1.5).astype(jnp.bfloat16)
    in_weight = gaussian(arg_keys[3], (D, PROJ), D ** -0.5, 0.21875, ((0, 32),))
    conv_weight = gaussian(arg_keys[4], (CONV, XBC), CONV ** -0.5, 3.0, ((1, 32),))
    conv_bias = jnp.clip(jax.random.uniform(arg_keys[5], (XBC,), jnp.float32, -0.5, 0.5) * level_of(arg_keys[5], (XBC,), ((0, 32),), -0.4, 0.0), -0.5, 0.5).astype(jnp.bfloat16)
    gate_gain = jnp.clip(1.0 + 0.1 * jax.random.normal(arg_keys[6], (E,), jnp.float32), 0.5, 1.5).astype(jnp.bfloat16)
    out_weight = gaussian(arg_keys[7], (E, D), E ** -0.5, 0.15625, ((0, 32),))
    step_bias = jnp.clip(jax.random.uniform(arg_keys[8], (H,), jnp.float32, -6.9, -2.3), -6.9, -2.3)
    decay_log = jnp.clip(jax.random.uniform(arg_keys[9], (H,), jnp.float32, 0.0, 2.77), 0.0, 2.77)
    skip_weight = jnp.clip(jax.random.uniform(arg_keys[10], (H,), jnp.float32, 0.5, 1.5), 0.5, 1.5)
    cotangent = gaussian(arg_keys[11], (SEQS, LEN, D), 1.0, 6.0, ((0, 32),))
    return {"hidden_in": hidden_in, "segment_ids": segment_ids, "norm_gain": norm_gain, "in_weight": in_weight, "conv_weight": conv_weight, "conv_bias": conv_bias, "gate_gain": gate_gain, "out_weight": out_weight, "step_bias": step_bias, "decay_log": decay_log, "skip_weight": skip_weight, "cotangent": cotangent}


EPSILON = 1e-05
HIGHEST = lax.Precision.HIGHEST

def rms_scale(features, gain):
    return features * lax.rsqrt(lax.optimization_barrier(jnp.mean(features * features, axis=-1, keepdims=True)) + EPSILON) * gain

def block_within(pieces):
    query_block, key_block, cum_block, seg_block, input_block = pieces
    scores = jnp.dot(query_block, key_block.T, precision=HIGHEST)
    positions = jnp.arange(seg_block.shape[0])
    allowed = (positions[:, None] >= positions[None, :]) & (seg_block[:, None] == seg_block[None, :])
    allowed = allowed[None, :, :]
    cum_heads = cum_block.T
    log_gap = jnp.where(allowed, cum_heads[:, :, None] - cum_heads[:, None, :], 0.0)
    mixing = jnp.where(allowed, scores[None, :, :] * jnp.exp(log_gap), 0.0)
    return jnp.einsum('hqk,khp->qhp', mixing, input_block, precision=HIGHEST)

def mixer(projected, conv_weight, conv_bias, gate_gain, step_bias, decay_log, skip_weight, seg_ids):
    inner_width = gate_gain.shape[0]
    head_count = step_bias.shape[0]
    head_width = inner_width // head_count
    state_width = (conv_bias.shape[0] - inner_width) // 2
    seq_len = projected.shape[0]
    block_len = BLOCK
    block_count = seq_len // block_len
    gate_part = projected[:, :inner_width]
    conv_input = projected[:, inner_width:2 * inner_width + 2 * state_width]
    step_raw = projected[:, 2 * inner_width + 2 * state_width:]
    convolved = conv_bias + conv_weight[0] * conv_input
    for offset in range(1, conv_weight.shape[0]):
        earlier = jnp.pad(conv_input, ((offset, 0), (0, 0)))[:seq_len]
        earlier_seg = jnp.pad(seg_ids, (offset, 0), constant_values=-1)[:seq_len]
        same_doc = jnp.where(earlier_seg == seg_ids, 1.0, 0.0)[:, None]
        convolved = convolved + conv_weight[offset] * earlier * same_doc
    activated = jax.nn.silu(convolved)
    values = activated[:, :inner_width].reshape(seq_len, head_count, head_width)
    key_rows = activated[:, inner_width:inner_width + state_width]
    query_rows = activated[:, inner_width + state_width:]
    step_size = jax.nn.softplus(step_raw + step_bias)
    log_decay = -jnp.exp(decay_log) * step_size
    scaled = values * step_size[:, :, None]
    query_blocks = query_rows.reshape(block_count, block_len, state_width)
    key_blocks = key_rows.reshape(block_count, block_len, state_width)
    cumulative = jnp.cumsum(log_decay.reshape(block_count, block_len, head_count), axis=1)
    seg_blocks = seg_ids.reshape(block_count, block_len)
    scaled_blocks = scaled.reshape(block_count, block_len, head_count, head_width)
    within = lax.map(block_within, (query_blocks, key_blocks, cumulative, seg_blocks, scaled_blocks))
    last_seg = seg_blocks[:, -1]
    last_cum = cumulative[:, -1, :]
    to_end = jnp.where((seg_blocks == last_seg[:, None])[:, :, None], jnp.exp(last_cum[:, None, :] - cumulative), 0.0)
    weighted = scaled_blocks * to_end[:, :, :, None]
    local_states = jnp.einsum('ckn,ckhp->chnp', key_blocks, weighted, precision=HIGHEST)
    carried = jnp.zeros_like(local_states[0])
    entering = []
    for block_index in range(block_count):
        entering.append(carried)
        if block_index == 0:
            carried = local_states[0]
        else:
            linked = jnp.where(last_seg[block_index - 1] == last_seg[block_index], 1.0, 0.0)
            carried = local_states[block_index] + linked * jnp.exp(last_cum[block_index])[:, None, None] * carried
    entering = jnp.stack(entering)
    prior_seg = jnp.concatenate([jnp.full((1,), -1, seg_ids.dtype), last_seg[:-1]])
    reaching = jnp.where((seg_blocks == prior_seg[:, None])[:, :, None], jnp.exp(cumulative), 0.0)
    across = jnp.einsum('cqn,chnp->cqhp', query_blocks, entering, precision=HIGHEST) * reaching[:, :, :, None]
    ssm_out = (within + across).reshape(seq_len, head_count, head_width) + skip_weight[:, None] * values
    gated_in = ssm_out.reshape(seq_len, inner_width) * jax.nn.silu(gate_part)
    return rms_scale(gated_in, gate_gain)

def forward_pass(hidden, seg_ids, weights, head_params):
    norm_gain, in_weight, conv_weight, conv_bias, gate_gain, out_weight = weights
    step_bias, decay_log, skip_weight = head_params
    features = hidden.astype(jnp.float32)
    normed = rms_scale(features, norm_gain.astype(jnp.float32)).astype(jnp.bfloat16)
    projected = jnp.dot(normed, in_weight, preferred_element_type=jnp.float32)

    def local_mixer(proj_in, conv_taps, conv_shift, gate_scale, bias_steps, decay_logs, skip_gains):
        return mixer(proj_in, conv_taps, conv_shift, gate_scale, bias_steps, decay_logs, skip_gains, seg_ids)
    mixed_out, mixer_back = jax.vjp(local_mixer, projected, conv_weight.astype(jnp.float32), conv_bias.astype(jnp.float32), gate_gain.astype(jnp.float32), step_bias, decay_log, skip_weight)
    gated = mixed_out.astype(jnp.bfloat16)
    output = (features + jnp.dot(gated, out_weight, preferred_element_type=jnp.float32)).astype(jnp.bfloat16)
    return (output, (features, normed, gated, mixer_back))

def backward_pass(cotangent, stored, weights):
    features, normed, gated, mixer_back = stored
    norm_gain, in_weight, conv_weight, conv_bias, gate_gain, out_weight = weights
    grad_out_weight = jnp.dot(gated.T, cotangent, preferred_element_type=jnp.float32)
    grad_gated = jnp.dot(cotangent, out_weight.T, preferred_element_type=jnp.float32)
    mixer_grads = mixer_back(grad_gated)
    rounded_grad = mixer_grads[0].astype(jnp.bfloat16)
    grad_in_weight = jnp.dot(normed.T, rounded_grad, preferred_element_type=jnp.float32)
    grad_normed = jnp.dot(rounded_grad, in_weight.T, preferred_element_type=jnp.float32)
    norm_value, norm_back = jax.vjp(rms_scale, features, norm_gain.astype(jnp.float32))
    grad_features, grad_norm_gain = norm_back(grad_normed)
    hidden_grad = (cotangent.astype(jnp.float32) + grad_features).astype(jnp.bfloat16)
    weight_part = (grad_norm_gain, grad_in_weight, mixer_grads[1], mixer_grads[2], mixer_grads[3], grad_out_weight)
    head_part = (mixer_grads[4], mixer_grads[5], mixer_grads[6])
    return (hidden_grad, weight_part, head_part)

def add_pair(first, second):
    return first + second

def reference(hidden_in, segment_ids, norm_gain, in_weight, conv_weight, conv_bias, gate_gain, out_weight, step_bias, decay_log, skip_weight, cotangent):
    weights = (norm_gain, in_weight, conv_weight, conv_bias, gate_gain, out_weight)
    head_params = (step_bias, decay_log, skip_weight)
    start = (tuple((jnp.zeros(piece.shape, jnp.float32) for piece in weights)), tuple((jnp.zeros(piece.shape, jnp.float32) for piece in head_params)))

    def one_sequence(totals, pieces):
        hidden, seg_ids, cot_rows = pieces
        output, stored = forward_pass(hidden, seg_ids, weights, head_params)
        hidden_grad, weight_part, head_part = backward_pass(cot_rows, stored, weights)
        totals = jax.tree.map(add_pair, totals, (weight_part, head_part))
        return (totals, (output, hidden_grad))
    totals, stacked = lax.scan(one_sequence, start, (hidden_in, segment_ids, cotangent))
    weight_sums, head_sums = totals
    return (stacked[0], stacked[1], weight_sums[0], weight_sums[1], weight_sums[2], weight_sums[3], weight_sums[4], weight_sums[5], head_sums[0], head_sums[1], head_sums[2])
```

```python
import jax
import jax.numpy as jnp
from jax import lax
from jax.experimental import pallas as pl
from jax.experimental.pallas import tpu as pltpu
from jax.sharding import PartitionSpec as P

AXES = ("dp", "fsdp")
EPSILON = 1e-05
LANES = 128
NEG = -1e30
F32 = jnp.float32
BF16 = jnp.bfloat16


def swap(value, mask, count):
    return lax.ppermute(value, AXES, [(i, i ^ mask) for i in range(count)])


def plan(count):
    bits = count.bit_length() - 1
    far = [list(range(b, min(b + 2, bits))) for b in range(3, bits, 2)]
    return bits, far


def bit_reverse(p, bits):
    return sum(((p >> b) & 1) << (bits - 1 - b) for b in range(bits))


def traced_bit_reverse(p, bits):
    out = jnp.zeros_like(p)
    for b in range(bits):
        out = out | (((p >> b) & 1) << (bits - 1 - b))
    return out


def gather_halves(shard, color, count):
    bits, far = plan(count)
    buf = shard
    for group in reversed(far):
        width = len(group)
        parts = []
        for pos in range(1 << width):
            mask = sum(((pos >> (width - 1 - k)) & 1) << group[k] for k in range(width))
            parts.append(buf if mask == 0 else swap(buf, mask, count))
        buf = jnp.stack(parts).reshape((2,) * width + buf.shape)
    if color == 0:
        buf = jnp.stack([buf, swap(buf, 4, count)])
        buf = jnp.stack([buf, swap(buf, 2, count)])
    else:
        buf = jnp.stack([buf, swap(buf, 2, count)])
        buf = jnp.stack([buf, swap(buf, 4, count)], axis=1)
    other = swap(buf, 1, count)
    flat = lambda v: v.reshape((-1,) + shard.shape[1:])
    return flat(buf), flat(other)


def scatter_halves(keep, send, color, count, rows):
    bits, far = plan(count)
    shape = (2,) * (bits - 1) + (rows, keep.shape[-1])
    add = lambda a, b: a.astype(F32) + b.astype(F32)
    got = swap(send.reshape(shape), 1, count)
    keep = keep.reshape(shape)
    if color == 0:
        got2 = swap(add(keep[1], got[1]).astype(BF16), 2, count)
        now = add(keep[0], got[0]).astype(BF16)
        got3 = swap(add(now[1], got2[1]).astype(BF16), 4, count)
        now = add(now[0], got2[0])
        now = now + got3.astype(F32)
    else:
        got2 = swap(add(keep[:, 1], got[:, 1]).astype(BF16), 4, count)
        now = add(keep[:, 0], got[:, 0]).astype(BF16)
        got3 = swap(add(now[1], got2[1]).astype(BF16), 2, count)
        now = add(now[0], got2[0])
        now = now + got3.astype(F32)
    for group in far:
        width = len(group)
        flat = now.reshape((1 << width,) + now.shape[width:])
        total = flat[0]
        low = flat.astype(BF16)
        for pos in range(1, 1 << width):
            mask = sum(((pos >> (width - 1 - k)) & 1) << group[k] for k in range(width))
            total = total + swap(low[pos], mask, count).astype(F32)
        now = total
    return now


def sum_everywhere(value, count):
    bits, far = plan(count)
    for group in [[0, 1, 2]] + far:
        parts = []
        for pos in range(1 << len(group)):
            mask = sum(((pos >> k) & 1) << group[k] for k in range(len(group)))
            parts.append(value if mask == 0 else swap(value, mask, count))
        while len(parts) > 1:
            parts = [parts[i] + parts[i + 1] for i in range(0, len(parts), 2)]
        value = parts[0]
    return value


def mm(a, b, ca=1, cb=0):
    return lax.dot_general(a, b, (((ca,), (cb,)), ((), ())), preferred_element_type=F32)


def split3(v):
    hi = v.astype(BF16)
    rest = v - hi.astype(F32)
    mid = rest.astype(BF16)
    low = (rest - mid.astype(F32)).astype(BF16)
    return hi, mid, low


def exact_mm(onehot, v):
    hi, mid, low = split3(v)
    return mm(onehot, hi) + mm(onehot, mid) + mm(onehot, low)


def iota(shape, dim):
    return lax.broadcasted_iota(jnp.int32, shape, dim)


def sigmoid(v):
    return 1.0 / (1.0 + jnp.exp(-v))


def softplus(u):
    return jnp.maximum(u, 0.0) + jnp.log1p(jnp.exp(-jnp.abs(u)))


def rows_of(v, k, n):
    return pltpu.roll(v, k % n, 0)


def conv_chunk(x, taps_ref, keep_ref, c0, taps):
    n = x.shape[0]
    acc = taps_ref[taps : taps + 1, c0 : c0 + LANES] + taps_ref[0:1, c0 : c0 + LANES] * x
    for k in range(1, taps):
        acc = acc + taps_ref[k : k + 1, c0 : c0 + LANES] * (rows_of(x, k, n) * keep_ref[k - 1])
    return acc


def fill_masks(cm_ref, keep_ref, taps):
    n = cm_ref.shape[0]
    for k in range(1, taps):
        keep_ref[k - 1] = jnp.broadcast_to(cm_ref[:, k : k + 1], (n, LANES))


def decay_tables(step_raw, heads_ref):
    n = step_raw.shape[0]
    u = step_raw + heads_ref[0:1, :]
    dt = softplus(u)
    rate = jnp.exp(heads_ref[1:2, :])
    ld = -rate * dt
    tri = jnp.where(iota((n, n), 0) >= iota((n, n), 1), 1.0, 0.0).astype(BF16)
    cum = exact_mm(tri, ld)
    return u, dt, rate, ld, cum


def pair_lanes(v, p):
    n = v.shape[0]
    left = iota((n, LANES), 1) < LANES // 2
    return jnp.where(left, v[:, 2 * p : 2 * p + 1], v[:, 2 * p + 1 : 2 * p + 2])


def forward_kernel(hid_ref, gain_ref, a0, a1, b0, b1, taps_ref, heads_ref, skip_ref, cm_ref,
                   segc_ref, segr_ref, normed_ref, xraw_ref, ssm_ref,
                   keep_ref, mask_ref, g_ref, cum_s, cumt_s, dt_s, *, inner, state, taps):
    n = hid_ref.shape[0]
    f = hid_ref[...].astype(F32)
    inv = lax.rsqrt(jnp.mean(f * f, axis=1, keepdims=True) + EPSILON)
    normed = (f * inv * gain_ref[...]).astype(BF16)
    normed_ref[...] = normed
    half = a0.shape[0]
    n0, n1 = normed[:, :half], normed[:, half:]
    wa = a0.shape[1]
    xraw_ref[:, :wa] = mm(n0, a0[...]) + mm(n1, a1[...])
    xraw_ref[:, wa:] = mm(n0, b0[...]) + mm(n1, b1[...])
    fill_masks(cm_ref, keep_ref, taps)
    chan = inner + 2 * state
    _, dt, _, _, cum = decay_tables(xraw_ref[:, chan : chan + LANES], heads_ref)
    cum_s[...] = cum
    cumt_s[...] = cum.T
    dt_s[...] = dt
    same = segc_ref[...] == segr_ref[0]
    mask_ref[...] = jnp.where(same & (iota((n, n), 0) >= iota((n, n), 1)), 0.0, NEG)

    def act(c0):
        v = conv_chunk(xraw_ref[:, c0 : c0 + LANES], taps_ref, keep_ref, c0, taps)
        return v / (1.0 + jnp.exp(-v))

    keys = act(inner).astype(BF16)
    queries = act(inner + state).astype(BF16)
    g_ref[...] = mm(queries, keys, 1, 1)
    left = iota((n, LANES), 1) < LANES // 2
    for p in range(inner // LANES):
        c0 = p * LANES
        x = act(c0)
        xt = (x * pair_lanes(dt_s[...], p)).astype(F32)
        out = None
        for side in range(2):
            h = 2 * p + side
            gap = (mask_ref[...] + cum_s[:, h : h + 1]) - cumt_s[h : h + 1, :]
            mix = (g_ref[...] * jnp.exp(gap)).astype(BF16)
            xs = jnp.where(left if side == 0 else ~left, xt, 0.0).astype(BF16)
            part = mm(mix, xs)
            out = part if out is None else out + part
        ssm_ref[:, c0 : c0 + LANES] = out + skip_ref[:, c0 : c0 + LANES] * x


def gate_kernel(me_ref, hid_ref, cot_ref, normed_ref, ssm_ref, gg_ref, za0, za1, zb0, zb1, w0, w1,
                out_ref, gated_ref, dy_ref, dz_ref, dgain_ref,
                w_s, z_s, g_s, sem, *, count, move):
    bits = count.bit_length() - 1
    inner = ssm_ref.shape[1]
    rows = inner // count
    n = ssm_ref.shape[0]

    def copies():
        for p in range(count):
            src = (w0 if p < count // 2 else w1).at[pl.ds((p % (count // 2)) * rows, rows)]
            spot = pl.multiple_of((me_ref[0] ^ bit_reverse(p, bits)) * rows, rows)
            yield pltpu.make_async_copy(src, w_s.at[pl.ds(spot, rows)], sem.at[p])

    if move:
        @pl.when(pl.program_id(0) == 0)
        def _():
            for c in copies():
                c.start()
    normed = normed_ref[...]
    half = za0.shape[0]
    n0, n1 = normed[:, :half], normed[:, half:]
    wa = za0.shape[1]
    z_s[:, :wa] = mm(n0, za0[...]) + mm(n1, za1[...])
    z_s[:, wa:] = mm(n0, zb0[...]) + mm(n1, zb1[...])
    acc = jnp.zeros((n, LANES), F32)
    for c0 in range(0, inner, LANES):
        z = z_s[:, c0 : c0 + LANES]
        g = ssm_ref[:, c0 : c0 + LANES] * (z / (1.0 + jnp.exp(-z)))
        g_s[:, c0 : c0 + LANES] = g
        acc = acc + g * g
    r = lax.rsqrt(jnp.sum(acc, axis=1, keepdims=True) / inner + EPSILON)
    for c0 in range(0, inner, LANES):
        gated_ref[:, c0 : c0 + LANES] = (
            g_s[:, c0 : c0 + LANES] * r * gg_ref[:, c0 : c0 + LANES]
        ).astype(BF16)
    if move:
        @pl.when(pl.program_id(0) == 0)
        def _():
            for c in copies():
                c.wait()
        weight = w_s[...]
    else:
        weight = w0[...]
    out_ref[...] = (hid_ref[...].astype(F32) + mm(gated_ref[...], weight)).astype(BF16)
    grad = mm(cot_ref[...], weight, 1, 1)

    @pl.when(pl.program_id(0) == 0)
    def _():
        dgain_ref[...] = jnp.zeros_like(dgain_ref)

    acc = jnp.zeros((n, LANES), F32)
    for c0 in range(0, inner, LANES):
        g = g_s[:, c0 : c0 + LANES]
        gr = grad[:, c0 : c0 + LANES]
        acc = acc + gr * gg_ref[:, c0 : c0 + LANES] * g
        dgain_ref[0:1, c0 : c0 + LANES] += jnp.sum(gr * (g * r), axis=0, keepdims=True)
    s = jnp.sum(acc, axis=1, keepdims=True) * (r * r * r) / inner
    for c0 in range(0, inner, LANES):
        z = z_s[:, c0 : c0 + LANES]
        sz = sigmoid(z)
        dg = grad[:, c0 : c0 + LANES] * gg_ref[:, c0 : c0 + LANES] * r - g_s[:, c0 : c0 + LANES] * s
        dy_ref[:, c0 : c0 + LANES] = (dg * (z * sz)).astype(BF16)
        dz_ref[:, c0 : c0 + LANES] = (
            dg * ssm_ref[:, c0 : c0 + LANES] * (sz * (1.0 + z * (1.0 - sz)))
        ).astype(BF16)


def out_grad_kernel(me_ref, gated_ref, cot_ref, out_ref, s_ref, sem, *, count):
    bits = count.bit_length() - 1
    rows = gated_ref.shape[1] // count
    s_ref[...] = mm(gated_ref[...], cot_ref[...], 0, 0).astype(BF16)
    pending = []
    for p in range(count):
        spot = pl.multiple_of((me_ref[0] ^ bit_reverse(p, bits)) * rows, rows)
        c = pltpu.make_async_copy(s_ref.at[pl.ds(spot, rows)], out_ref.at[pl.ds(p * rows, rows)], sem.at[p])
        c.start()
        pending.append(c)
    for c in pending:
        c.wait()


def backward_kernel(xraw_ref, ssm_ref, dy_ref, taps_ref, heads_ref, skip_ref, cm_ref, segc_ref, segr_ref,
                    dx_ref, conv_ref, head_ref,
                    keep_ref, mask_ref, gt_ref, dgt_ref, cum_s, cumt_s, dt_s, dcum_s, ddt_s,
                    *, inner, state, taps):
    n = xraw_ref.shape[0]
    fill_masks(cm_ref, keep_ref, taps)
    chan = inner + 2 * state
    u, dt, rate, ld, cum = decay_tables(xraw_ref[:, chan : chan + LANES], heads_ref)
    cum_s[...] = cum
    cumt_s[...] = cum.T
    dt_s[...] = dt
    same = segc_ref[...] == segr_ref[0]
    mask_ref[...] = jnp.where(same & (iota((n, n), 1) >= iota((n, n), 0)), 0.0, NEG)

    @pl.when(pl.program_id(0) == 0)
    def _():
        conv_ref[...] = jnp.zeros_like(conv_ref)
        head_ref[...] = jnp.zeros_like(head_ref)

    def act(c0):
        v = conv_chunk(xraw_ref[:, c0 : c0 + LANES], taps_ref, keep_ref, c0, taps)
        s = sigmoid(v)
        return v * s, s * (1.0 + v * (1.0 - s))

    def conv_back(c0, dv):
        x = xraw_ref[:, c0 : c0 + LANES]
        out = taps_ref[0:1, c0 : c0 + LANES] * dv
        conv_ref[0:1, c0 : c0 + LANES] += jnp.sum(dv * x, axis=0, keepdims=True)
        for k in range(1, taps):
            w = rows_of(dv * keep_ref[k - 1], -k, n)
            out = out + taps_ref[k : k + 1, c0 : c0 + LANES] * w
            conv_ref[k : k + 1, c0 : c0 + LANES] += jnp.sum(w * x, axis=0, keepdims=True)
        conv_ref[taps : taps + 1, c0 : c0 + LANES] += jnp.sum(dv, axis=0, keepdims=True)
        dx_ref[:, c0 : c0 + LANES] = out.astype(BF16)

    kact, kslope = act(inner)
    qact, qslope = act(inner + state)
    keys, queries = kact.astype(BF16), qact.astype(BF16)
    gt_ref[...] = mm(keys, queries, 1, 1)
    dgt_ref[...] = jnp.zeros_like(dgt_ref)
    dcum_s[...] = jnp.zeros_like(dcum_s)
    ddt_s[...] = jnp.zeros_like(ddt_s)
    left = iota((n, LANES), 1) < LANES // 2
    for p in range(inner // LANES):
        c0 = p * LANES
        x, slope = act(c0)
        dtp = pair_lanes(dt_s[...], p)
        xb = (x * dtp).astype(BF16)
        xf = xb.astype(F32)
        dy = dy_ref[:, c0 : c0 + LANES]
        dyf = dy.astype(F32)
        dxt = None
        for side in range(2):
            h = 2 * p + side
            lanes = left if side == 0 else ~left
            e = jnp.exp((mask_ref[...] + cumt_s[h : h + 1, :]) - cum_s[:, h : h + 1])
            mix = (gt_ref[...] * e).astype(BF16)
            part = mm(mix, jnp.where(lanes, dyf, 0.0).astype(BF16))
            dxt = part if dxt is None else dxt + part
            dmix = mm(jnp.where(lanes, xf, 0.0).astype(BF16), dy, 1, 1)
            dgt_ref[...] += dmix * e
        skip = skip_ref[:, c0 : c0 + LANES]
        within = ssm_ref[:, c0 : c0 + LANES] - skip * x
        pick = jnp.where(iota((LANES, LANES), 0) // (LANES // 2) + 2 * p == iota((LANES, LANES), 1), 1.0, 0.0).astype(BF16)
        for ref, v in ((dcum_s, dyf * within - xf * dxt), (ddt_s, dxt * x)):
            hi, mid, low = split3(v)
            ref[...] += mm(hi, pick) + mm(mid, pick) + mm(low, pick)
        conv_ref[taps + 1 : taps + 2, c0 : c0 + LANES] += jnp.sum(dyf * x, axis=0, keepdims=True)
        conv_back(c0, (dxt * dtp + skip * dyf) * slope)
    dgt = dgt_ref[...].astype(BF16)
    conv_back(inner, mm(dgt, queries) * kslope)
    conv_back(inner + state, mm(dgt, keys, 0, 0) * qslope)
    later = jnp.where(iota((n, n), 1) >= iota((n, n), 0), 1.0, 0.0).astype(BF16)
    dld = exact_mm(later, dcum_s[...])
    dstep = (ddt_s[...] - rate * dld) * sigmoid(u)
    dx_ref[:, chan : chan + LANES] = dstep.astype(BF16)
    head_ref[0:1, :] += jnp.sum(dstep, axis=0, keepdims=True)
    head_ref[1:2, :] += jnp.sum(ld * dld, axis=0, keepdims=True)


def input_grad_kernel(hid_ref, cot_ref, gain_ref, dz_ref, dx_ref, za0, za1, zb0, zb1, a0, a1, b0, b1,
                      out_ref, dgain_ref):
    half = za0.shape[0]
    wz, wx = za0.shape[1], a0.shape[1]
    dza, dzb, dxa, dxb = dz_ref[:, :wz], dz_ref[:, wz:], dx_ref[:, :wx], dx_ref[:, wx:]
    f = hid_ref[...].astype(F32)
    inv = lax.rsqrt(jnp.mean(f * f, axis=1, keepdims=True) + EPSILON)

    @pl.when(pl.program_id(0) == 0)
    def _():
        dgain_ref[...] = jnp.zeros_like(dgain_ref)

    total = jnp.zeros((f.shape[0], 1), F32)
    pieces = []
    for side, (p, q, r, s) in enumerate(((za0, zb0, a0, b0), (za1, zb1, a1, b1))):
        cols = slice(side * half, (side + 1) * half)
        dn = mm(dza, p[...], 1, 1) + mm(dzb, q[...], 1, 1) + mm(dxa, r[...], 1, 1) + mm(dxb, s[...], 1, 1)
        fs = f[:, cols]
        dgain_ref[0:1, cols] += jnp.sum(dn * (fs * inv), axis=0, keepdims=True)
        a = dn * gain_ref[:, cols]
        total = total + jnp.sum(a * fs, axis=1, keepdims=True)
        pieces.append(a)
    scale = total * (inv * inv * inv) / f.shape[1]
    for side, a in enumerate(pieces):
        cols = slice(side * half, (side + 1) * half)
        out_ref[:, cols] = (cot_ref[:, cols].astype(F32) + a * inv - f[:, cols] * scale).astype(BF16)


def call(kernel, args, in_specs, outs, out_specs, scratch, grid, flops, name):
    size = sum(a.size * a.dtype.itemsize for a in args) + sum(a.size * a.dtype.itemsize for a in outs)
    return pl.pallas_call(
        kernel,
        grid_spec=pltpu.PrefetchScalarGridSpec(
            num_scalar_prefetch=0, grid=grid, in_specs=in_specs, out_specs=out_specs, scratch_shapes=scratch
        ),
        out_shape=outs,
        cost_estimate=pl.CostEstimate(flops=flops, transcendentals=0, bytes_accessed=size),
        compiler_params=pltpu.CompilerParams(vmem_limit_bytes=60 * 1024 * 1024),
        name=name,
    )(*args)


def on_device(hidden_in, segment_ids, norm_gain, in_weight, conv_weight, conv_bias, gate_gain, out_weight,
              step_bias, decay_log, skip_weight, cotangent):
    count = lax.psum(1, AXES)
    bits, _ = plan(count)
    me = lax.axis_index(AXES)
    length, width = hidden_in.shape[1:]
    drow = in_weight.shape[0]
    erow = out_weight.shape[0]
    inner = erow * count
    taps = conv_weight.shape[0]
    xbc = conv_bias.shape[0] * count
    state = (xbc - inner) // 2
    heads = step_bias.shape[0]
    n = length // 2
    blocks = length // n
    pad = LANES - heads

    small = jnp.concatenate([norm_gain, conv_bias, gate_gain, conv_weight.reshape(-1)])
    s0, s1 = gather_halves(small[None, :], 0, count)
    cut = inner + (xbc // 2 + LANES - 1) // LANES * LANES
    wxa = in_weight[:, inner:cut]
    wxb = jnp.pad(in_weight[:, cut:], ((0, 0), (0, pad)))
    a0, a1 = gather_halves(wxa, 0, count)
    b0, b1 = gather_halves(wxb, 1, count)
    za0, za1 = gather_halves(in_weight[:, : inner // 2], 0, count)
    zb0, zb1 = gather_halves(in_weight[:, inner // 2 : inner], 1, count)
    ca = erow // 2
    wo = gather_halves(out_weight, 0, count)

    spots = me ^ traced_bit_reverse(jnp.arange(count), bits)
    small_rel = jnp.concatenate([s0, s1])
    own = (spots[None, :] == jnp.arange(count)[:, None]).astype(BF16)
    small_all = jnp.dot(own, small_rel, preferred_element_type=F32)
    gain_rel = small_rel[:, :drow].reshape(1, width).astype(F32)
    c1 = drow + conv_bias.shape[0]
    c2 = c1 + erow
    bias_all = small_all[:, drow:c1].reshape(1, xbc)
    gate_all = small_all[:, c1:c2].reshape(1, inner)
    taps_all = small_all[:, c2:].reshape(count, taps, -1).transpose(1, 0, 2).reshape(taps, xbc)
    taps_in = jnp.pad(jnp.concatenate([taps_all, bias_all]), ((0, 8 - taps - 1), (0, 0)))
    heads_in = jnp.pad(jnp.stack([step_bias, decay_log]), ((0, 6), (0, pad)))
    skip_in = jnp.repeat(skip_weight, inner // heads).reshape(1, inner)

    seg = segment_ids[0]
    n0 = jnp.sum((seg == 0).astype(jnp.int32))
    n1 = jnp.sum((seg == 1).astype(jnp.int32))
    shift = jnp.where(n1 == n, n0, 0)
    at = (jnp.arange(length) + shift) % length
    seg_rot = (at >= n0).astype(jnp.int32) + (at >= n0 + n1).astype(jnp.int32)
    turn = (at[:, None] == jnp.arange(length)[None, :]).astype(BF16)
    place = (jnp.arange(width) // drow)
    source = jnp.repeat(spots, drow) * drow + jnp.arange(width) % drow
    chans = (jnp.arange(width)[:, None] == source[None, :]).astype(BF16)
    exact = lambda a, b: jnp.dot(a, b, preferred_element_type=F32).astype(BF16)
    hid_r = exact(turn, hidden_in[0])
    cot_r = exact(turn, cotangent[0])
    hid_p = exact(hid_r, chans)
    cot_p = exact(cot_r, chans)
    seg_b = seg_rot.reshape(blocks, n)
    lag = [jnp.pad(seg_b, ((0, 0), (k, 0)), constant_values=-1)[:, :n] == seg_b for k in range(taps)]
    cm = jnp.pad(jnp.stack(lag, axis=-1).astype(F32).reshape(length, taps), ((0, 0), (0, 8 - taps)))
    seg_col = seg_rot.reshape(length, 1)
    seg_row = seg_b.reshape(blocks, 1, n)

    rowblock = lambda c: pl.BlockSpec((n, c), lambda i: (i, 0))
    whole = lambda a: pl.BlockSpec(a.shape, lambda i: (0,) * a.ndim)
    segspec = pl.BlockSpec((1, 1, n), lambda i: (i, 0, 0))
    vm = lambda *s: pltpu.VMEM(s, F32)
    sds = jax.ShapeDtypeStruct
    wide = xbc + LANES
    square = 2 * n * n

    args = (hid_p, gain_rel, a0, a1, b0, b1, taps_in, heads_in, skip_in, cm, seg_col, seg_row)
    normed, xraw, ssm = call(
        lambda *r: forward_kernel(*r, inner=inner, state=state, taps=taps),
        args,
        [rowblock(width)] + [whole(v) for v in args[1:9]] + [rowblock(8), rowblock(1), segspec],
        (sds((length, width), BF16), sds((length, wide), F32), sds((length, inner), F32)),
        (rowblock(width), rowblock(wide), rowblock(inner)),
        [vm(taps - 1, n, LANES), vm(n, n), vm(n, n), vm(n, LANES), vm(LANES, n), vm(n, LANES)],
        (blocks,), 2 * length * width * wide + blocks * heads * square * LANES, "mixer_forward",
    )

    me1 = me.reshape(1).astype(jnp.int32)
    move = erow % 16 == 0
    if move:
        w0, w1 = wo
        wspec = pl.BlockSpec(memory_space=pl.ANY)
    else:
        w0 = jnp.take(jnp.concatenate(wo).reshape(count, erow, width), traced_bit_reverse(me ^ jnp.arange(count), bits), axis=0)
        w0 = w0.reshape(inner, width)
        w1 = me1
        wspec = None
    smem = pl.BlockSpec(memory_space=pltpu.SMEM)
    args = (me1, hid_r, cot_r, normed, ssm, gate_all, za0, za1, zb0, zb1, w0, w1)
    out_rot, gated, dy, dz, dgate = call(
        lambda *r: gate_kernel(*r, count=count, move=move),
        args,
        [smem, rowblock(width), rowblock(width), rowblock(width), rowblock(inner)]
        + [whole(v) for v in args[5:10]] + ([wspec, wspec] if move else [whole(w0), smem]),
        (sds((length, width), BF16), sds((length, inner), BF16), sds((length, inner), BF16),
         sds((length, inner), BF16), sds((8, inner), F32)),
        (rowblock(width), rowblock(inner), rowblock(inner), rowblock(inner), pl.BlockSpec((8, inner), lambda i: (0, 0))),
        [pltpu.VMEM((inner, width), BF16), vm(n, inner), vm(n, inner), pltpu.SemaphoreType.DMA((count,))],
        (blocks,), 3 * 2 * length * width * inner, "gate",
    )

    if move:
        gow = call(
            lambda *r: out_grad_kernel(*r, count=count), (me1, gated, cot_r),
            [smem, whole(gated), whole(cot_r)], (sds((inner, width), BF16),), (pl.BlockSpec(memory_space=pl.ANY),),
            [pltpu.VMEM((inner, width), BF16), pltpu.SemaphoreType.DMA((count,))],
            (1,), 2 * length * width * inner, "out_grad",
        )[0]
    else:
        gow = lax.dot_general(gated, cot_r, (((0,), (0,)), ((), ())), preferred_element_type=F32).astype(BF16)
        gow = jnp.take(gow.reshape(count, erow, width), spots, axis=0).reshape(inner, width)
    hrow = inner // 2
    grad_out_weight = scatter_halves(gow[:hrow], gow[hrow:], 0, count, erow)

    half = width // 2

    def weight_grad(g, color):
        parts = [
            lax.dot_general(normed[:, i * half : (i + 1) * half], g, (((0,), (0,)), ((), ())), preferred_element_type=F32).astype(BF16)
            for i in range(2)
        ]
        return scatter_halves(parts[0], parts[1], color, count, drow)

    gz = [weight_grad(dz[:, : inner // 2], 0), weight_grad(dz[:, inner // 2 :], 1)]

    args = (xraw, ssm, dy, taps_in, heads_in, skip_in, cm, seg_col, seg_row)
    dxbc, conv_sums, head_sums = call(
        lambda *r: backward_kernel(*r, inner=inner, state=state, taps=taps),
        args,
        [rowblock(wide), rowblock(inner), rowblock(inner)] + [whole(v) for v in args[3:6]]
        + [rowblock(8), rowblock(1), segspec],
        (sds((length, wide), BF16), sds((8, wide), F32), sds((8, LANES), F32)),
        (rowblock(wide), pl.BlockSpec((8, wide), lambda i: (0, 0)), pl.BlockSpec((8, LANES), lambda i: (0, 0))),
        [vm(taps - 1, n, LANES), vm(n, n), vm(n, n), vm(n, n), vm(n, LANES), vm(LANES, n), vm(n, LANES),
         vm(n, LANES), vm(n, LANES)],
        (blocks,), blocks * heads * square * LANES * 2, "mixer_backward",
    )
    ca = cut - inner
    gx = [weight_grad(dxbc[:, :ca], 0), weight_grad(dxbc[:, ca:], 1)]

    args = (hid_p, cot_p, gain_rel, dz, dxbc, za0, za1, zb0, zb1, a0, a1, b0, b1)
    hg, dgain = call(
        input_grad_kernel, args,
        [rowblock(width), rowblock(width), whole(gain_rel), rowblock(inner), rowblock(wide)] + [whole(v) for v in args[5:]],
        (sds((length, width), BF16), sds((8, width), F32)),
        (rowblock(width), pl.BlockSpec((8, width), lambda i: (0, 0))),
        [], (blocks,), 2 * length * width * (inner + wide), "input_grad",
    )
    back = lambda v: lax.dot_general(turn, v, (((0,), (0,)), ((), ())), preferred_element_type=F32).astype(BF16)
    layer_out = back(out_rot)
    hidden_grad = back(lax.dot_general(hg, chans, (((1,), (1,)), ((), ())), preferred_element_type=F32).astype(BF16))

    dgain_nat = jnp.dot(own, dgain[0].reshape(count, drow), precision=lax.Precision.HIGHEST)
    skip_sum = conv_sums[taps + 1, :inner].reshape(heads, -1).sum(axis=1)
    flat = jnp.concatenate([
        dgain_nat.reshape(-1), dgate[0], conv_sums[: taps + 1, :xbc].reshape(-1),
        head_sums[0, :heads], head_sums[1, :heads], skip_sum,
    ])
    total = flat.shape[0]
    flat = jnp.pad(flat, (0, -total % 1024)).reshape(-1, LANES)
    flat = sum_everywhere(flat, count).reshape(-1)
    o1 = width + inner
    o2 = o1 + xbc * (taps + 1)
    mine = lambda v, size: lax.dynamic_slice_in_dim(v, me * size, size, axis=-1)
    conv_tot = mine(flat[o1:o2].reshape(taps + 1, xbc), xbc // count)
    return (
        layer_out[None],
        hidden_grad[None],
        mine(flat[:width], drow),
        jnp.concatenate(gz + [gx[0], gx[1][:, : gx[1].shape[1] - pad]], axis=1),
        conv_tot[:taps],
        conv_tot[taps],
        mine(flat[width:o1], erow),
        grad_out_weight,
        flat[o2 : o2 + heads],
        flat[o2 + heads : o2 + 2 * heads],
        flat[o2 + 2 * heads : o2 + 3 * heads],
    )


def solution(mesh):
    rows = P(AXES, None)
    placed = (
        P(AXES, None, None), rows, P(AXES), rows, P(None, AXES), P(AXES), P(AXES), rows,
        P(), P(), P(), P(AXES, None, None),
    )
    return jax.shard_map(
        on_device,
        mesh=mesh,
        in_specs=placed,
        out_specs=(
            P(AXES, None, None), P(AXES, None, None), P(AXES), rows, P(None, AXES), P(AXES), P(AXES), rows,
            P(), P(), P(),
        ),
        check_vma=False,
    )
```

```python
import jax
import jax.numpy as jnp
from jax import lax
from jax.experimental import pallas as pl
from jax.experimental.pallas import tpu as pltpu
from jax.sharding import PartitionSpec as P


AXES = ("dp", "fsdp")
EPSILON = 1e-05
LANES = 128
NEG = -1e30
F32 = jnp.float32
BF16 = jnp.bfloat16


def swap(value, mask, count):
    return lax.ppermute(value, AXES, [(i, i ^ mask) for i in range(count)])


def plan(count):
    bits = count.bit_length() - 1
    far = [list(range(b, min(b + 2, bits))) for b in range(3, bits, 2)]
    return bits, far


def bit_reverse(p, bits):
    return sum(((p >> b) & 1) << (bits - 1 - b) for b in range(bits))


def traced_bit_reverse(p, bits):
    out = jnp.zeros_like(p)
    for b in range(bits):
        out = out | (((p >> b) & 1) << (bits - 1 - b))
    return out


def masks_of(group):
    width = len(group)
    return [sum(((pos >> (width - 1 - k)) & 1) << group[k] for k in range(width)) for pos in range(1 << width)]


def far_gather(buf, count):
    for group in reversed(plan(count)[1]):
        parts = [swap(buf, m, count) if m else buf for m in masks_of(group)]
        buf = jnp.stack(parts).reshape((2,) * len(group) + buf.shape)
    return buf


def near_gather(left, right, count):
    got_l, got_r = swap(left, 4, count), swap(right, 2, count)
    left, right = jnp.stack([left, got_l]), jnp.stack([right, got_r])
    got_l, got_r = swap(left, 2, count), swap(right, 4, count)
    return jnp.stack([left, got_l]), jnp.stack([right, got_r], axis=1)


def small_gather(row, count):
    buf = jnp.concatenate([swap(row, m, count) if m else row for m in range(8)])
    for group in plan(count)[1]:
        masks = [sum(((pos >> k) & 1) << group[k] for k in range(len(group))) for pos in range(1 << len(group))]
        buf = jnp.concatenate([swap(buf, m, count) if m else buf for m in masks])
    return buf


def near_scatter(left, right, count):
    got_l = swap(left(1, slice(None)).astype(BF16), 2, count)
    got_r = swap(right(slice(None), 1).astype(BF16), 4, count)
    keep_l, keep_r = left(0, slice(None)), right(slice(None), 0)
    back_l = swap((keep_l[1] + got_l[1].astype(F32)).astype(BF16), 4, count)
    back_r = swap((keep_r[1] + got_r[1].astype(F32)).astype(BF16), 2, count)
    now_l = keep_l[0] + got_l[0].astype(F32) + back_l.astype(F32)
    now_r = keep_r[0] + got_r[0].astype(F32) + back_r.astype(F32)
    return jnp.concatenate([now_l, now_r], axis=-1)


def far_scatter(now, count):
    for group in plan(count)[1]:
        width = len(group)
        flat = now.reshape((1 << width,) + now.shape[width:])
        total = flat[0]
        got = [swap(flat[pos].astype(BF16), m, count) for pos, m in enumerate(masks_of(group)) if m]
        for g in got:
            total = total + g.astype(F32)
        now = total
    return now


def sum_everywhere(value, count):
    for group in [[0], [1, 2]] + plan(count)[1]:
        parts = []
        for pos in range(1 << len(group)):
            mask = sum(((pos >> k) & 1) << group[k] for k in range(len(group)))
            parts.append(value if mask == 0 else swap(value, mask, count))
        while len(parts) > 1:
            parts = [parts[i] + parts[i + 1] for i in range(0, len(parts), 2)]
        value = parts[0]
    return value


def mm(a, b, ca=1, cb=0):
    return lax.dot_general(a, b, (((ca,), (cb,)), ((), ())), preferred_element_type=F32)


def split3(v):
    hi = v.astype(BF16)
    rest = v - hi.astype(F32)
    mid = rest.astype(BF16)
    low = (rest - mid.astype(F32)).astype(BF16)
    return hi, mid, low


def exact_mm(onehot, v):
    hi, mid, low = split3(v)
    return mm(onehot, hi) + mm(onehot, mid) + mm(onehot, low)


def iota(shape, dim):
    return lax.broadcasted_iota(jnp.int32, shape, dim)


def sigmoid(v):
    return 1.0 / (1.0 + jnp.exp(-v))


def softplus(u):
    return jnp.maximum(u, 0.0) + jnp.log1p(jnp.exp(-jnp.abs(u)))


def rows_of(v, k, n):
    return pltpu.roll(v, k % n, 0)


def conv_chunk(x, taps_ref, keep_ref, c0, taps):
    n = x.shape[0]
    acc = taps_ref[taps : taps + 1, c0 : c0 + LANES] + taps_ref[0:1, c0 : c0 + LANES] * x
    for k in range(1, taps):
        acc = acc + taps_ref[k : k + 1, c0 : c0 + LANES] * (rows_of(x, k, n) * keep_ref[k - 1])
    return acc


def fill_masks(cm_ref, keep_ref, taps):
    n = cm_ref.shape[0]
    for k in range(1, taps):
        keep_ref[k - 1] = jnp.broadcast_to(cm_ref[:, k : k + 1], (n, LANES))


def decay_tables(step_raw, heads_ref):
    n = step_raw.shape[0]
    u = step_raw + heads_ref[0:1, :]
    dt = softplus(u)
    rate = jnp.exp(heads_ref[1:2, :])
    ld = -rate * dt
    tri = jnp.where(iota((n, n), 0) >= iota((n, n), 1), 1.0, 0.0).astype(BF16)
    cum = exact_mm(tri, ld)
    return u, dt, rate, ld, cum


def pair_lanes(v, p):
    n = v.shape[0]
    left = iota((n, LANES), 1) < LANES // 2
    return jnp.where(left, v[:, 2 * p : 2 * p + 1], v[:, 2 * p + 1 : 2 * p + 2])


def prep_kernel(me_ref, e0_ref, e1_ref, taps_ref, gate_ref, gain_ref, t_s, *, count, bits, first, sizes):
    drow = e0_ref.shape[0] * 2 // count
    taps, cwidth, erow = sizes
    table = jnp.concatenate([e0_ref[...], e1_ref[...]], axis=0)
    row = iota((8 * count, drow * count), 0)
    col = iota((8 * count, drow * count), 1)
    owner = row // 8
    rel = owner ^ me_ref[0]
    spot = jnp.zeros_like(rel)
    for b in range(bits):
        spot = spot | (((rel >> b) & 1) << (bits - 1 - b))
    pick = jnp.where(col == spot * drow + row % 8, 1.0, 0.0).astype(BF16)
    t_s[...] = pltpu.roll(mm(pick, table), LANES - first, 1)
    taps_ref[...] = jnp.zeros_like(taps_ref)
    for d in range(count):
        taps_ref[0 : taps + 1, d * cwidth : (d + 1) * cwidth] = t_s[d * 8 : d * 8 + taps + 1, :cwidth]
        gate_ref[0:1, d * erow : (d + 1) * erow] = t_s[d * 8 + taps + 1 : d * 8 + taps + 2, :erow]
    for p in range(count):
        line = (e0_ref if p < count // 2 else e1_ref)[
            (p % (count // 2)) * drow : (p % (count // 2)) * drow + 8, :].astype(F32)
        gain_ref[0:1, p * drow : (p + 1) * drow] = pltpu.roll(line, LANES - first, 1)[taps + 2 : taps + 3, :drow]


def forward_kernel(hid_ref, gain_ref, a0, a1, taps_ref, heads_ref, cm_ref,
                   segc_ref, segr_ref, *rest, inner, state, taps):
    normed_ref, xraw_ref, step_ref, xact_ref, slope_ref, y_ref = rest[-13:-7]
    raw_s, keep_ref, mask_ref, g_ref, cum_s, cumt_s, dt_s = rest[-7:]
    n = hid_ref.shape[0]
    t = n // 2
    f = hid_ref[...].astype(F32)
    inv = lax.rsqrt(jnp.mean(f * f, axis=1, keepdims=True) + EPSILON)
    normed = (f * inv * gain_ref[...]).astype(BF16)
    normed_ref[...] = normed
    half = a0.shape[0]
    raw_s[...] = mm(normed[:, :half], a0[...]) + mm(normed[:, half:], a1[...])
    fill_masks(cm_ref, keep_ref, taps)
    chan = inner + 2 * state
    step_ref[...] = raw_s[:, chan : chan + LANES]
    _, dt, _, _, cum = decay_tables(raw_s[:, chan : chan + LANES], heads_ref)
    cum_s[...] = cum
    cumt_s[...] = cum.T
    dt_s[...] = dt
    same = segc_ref[...] == segr_ref[0]
    mask_ref[...] = jnp.where(same & (iota((n, n), 0) >= iota((n, n), 1)), 0.0, NEG)

    def act(c0):
        raw = raw_s[:, c0 : c0 + LANES]
        xraw_ref[:, c0 : c0 + LANES] = raw.astype(BF16)
        v = conv_chunk(raw, taps_ref, keep_ref, c0, taps)
        s = sigmoid(v)
        x = v * s
        slope_ref[:, c0 : c0 + LANES] = (s + x * (1.0 - s)).astype(BF16)
        x = x.astype(BF16)
        xact_ref[:, c0 : c0 + LANES] = x
        return x

    keys = act(inner)
    queries = act(inner + state)
    g_ref[...] = mm(queries, keys, 1, 1)
    left = iota((n, LANES), 1) < LANES // 2
    for p in range(inner // LANES):
        c0 = p * LANES
        xt = act(c0).astype(F32) * pair_lanes(dt_s[...], p)
        top, bottom = None, None
        for side in range(2):
            h = 2 * p + side
            xs = jnp.where(left if side == 0 else ~left, xt, 0.0).astype(BF16)
            gap = (mask_ref[:t, :t] + cum_s[:t, h : h + 1]) - cumt_s[h : h + 1, :t]
            one = mm((g_ref[:t, :t] * jnp.exp(gap)).astype(BF16), xs[:t])
            gap = (mask_ref[t:, :] + cum_s[t:, h : h + 1]) - cumt_s[h : h + 1, :]
            two = mm((g_ref[t:, :] * jnp.exp(gap)).astype(BF16), xs)
            top = one if top is None else top + one
            bottom = two if bottom is None else bottom + two
        y_ref[:t, c0 : c0 + LANES] = top
        y_ref[t:, c0 : c0 + LANES] = bottom


def gate_kernel(me_ref, hid_ref, cot_ref, normed_ref, y_ref, xact_ref, gg_ref, skip_ref, za0, za1, w0, w1,
                out_ref, gated_ref, dy_ref, dz_ref, dgain_ref,
                w_s, z_s, g_s, h_s, r_s, sem, *, count, move):
    bits = count.bit_length() - 1
    inner = y_ref.shape[1]
    rows = inner // count
    n = y_ref.shape[0]
    step = 2 * LANES

    def copies():
        for p in range(count):
            src = (w0 if p < count // 2 else w1).at[pl.ds((p % (count // 2)) * rows, rows)]
            spot = pl.multiple_of((me_ref[0] ^ bit_reverse(p, bits)) * rows, rows)
            yield pltpu.make_async_copy(src, w_s.at[pl.ds(spot, rows)], sem.at[p])

    if move:
        @pl.when(pl.program_id(0) == 0)
        def _():
            for c in copies():
                c.start()

    @pl.when(pl.program_id(0) == 0)
    def _():
        dgain_ref[...] = jnp.zeros_like(dgain_ref)

    half = za0.shape[0]
    n0, n1 = normed_ref[:, :half], normed_ref[:, half:]
    acc = jnp.zeros((n, step), F32)
    for c0 in range(0, inner, step):
        cols = slice(c0, c0 + step)
        z = mm(n0, za0[:, cols]) + mm(n1, za1[:, cols])
        sz = sigmoid(z)
        zs = z * sz
        ssm = y_ref[:, cols] + skip_ref[:, cols] * xact_ref[:, cols].astype(F32)
        g = ssm * zs
        z_s[:, cols] = zs
        g_s[:, cols] = g
        h_s[:, cols] = ssm * (sz + zs * (1.0 - sz))
        acc = acc + g * g
    r = lax.rsqrt(jnp.sum(acc, axis=1, keepdims=True) / inner + EPSILON)
    if move:
        @pl.when(pl.program_id(0) == 0)
        def _():
            for c in copies():
                c.wait()

        w = w_s
    else:
        w = w0
    acc = jnp.zeros((n, step), F32)
    for c0 in range(0, inner, step):
        cols = slice(c0, c0 + step)
        grad = mm(cot_ref[...], w[cols, :], 1, 1)
        g = g_s[:, cols]
        gated = g * r
        gated_ref[:, cols] = (gated * gg_ref[:, cols]).astype(BF16)
        dgain_ref[0:1, cols] += jnp.sum(grad * gated, axis=0, keepdims=True)
        grad = grad * gg_ref[:, cols]
        r_s[:, cols] = grad
        acc = acc + grad * g
    s = jnp.sum(acc, axis=1, keepdims=True) * (r * r * r) / inner
    out_ref[...] = (hid_ref[...].astype(F32) + mm(gated_ref[...], w[...])).astype(BF16)
    for c0 in range(0, inner, step):
        cols = slice(c0, c0 + step)
        dg = r_s[:, cols] * r - g_s[:, cols] * s
        dy_ref[:, cols] = (dg * z_s[:, cols]).astype(BF16)
        dz_ref[:, cols] = (dg * h_s[:, cols]).astype(BF16)


def out_grad_kernel(me_ref, gated_ref, cot_ref, keep_ref, send_ref, s_ref, sem, *, count):
    bits = count.bit_length() - 1
    rows = gated_ref.shape[1] // count
    s_ref[...] = mm(gated_ref[...], cot_ref[...], 0, 0).astype(BF16)
    pending = []
    for p in range(count):
        spot = pl.multiple_of((me_ref[0] ^ bit_reverse(p, bits)) * rows, rows)
        dst = (keep_ref if p < count // 2 else send_ref).at[pl.ds((p % (count // 2)) * rows, rows)]
        c = pltpu.make_async_copy(s_ref.at[pl.ds(spot, rows)], dst, sem.at[p])
        c.start()
        pending.append(c)
    for c in pending:
        c.wait()


def backward_kernel(xact_m, xact_t, slope_m, slope_t, xraw_m, xraw_t, y_ref, dy_ref, step_ref,
                    taps_ref, heads_ref, skip_ref, cm_ref, segc_ref, segr_ref,
                    *rest, inner, state, taps, part, parts):
    dx_ref, conv_ref, head_ref, dgt_ref, dcum_s, ddt_s = rest[-12:-6]
    keep_ref, mask_ref, gt_ref, cum_s, cumt_s, dt_s = rest[-6:]
    first, last = part == 0, part == parts - 1
    carried = rest[: len(rest) - 12][-3:]
    n = y_ref.shape[0]
    t = n // 2
    fill_masks(cm_ref, keep_ref, taps)
    chan = inner + 2 * state
    u, dt, rate, ld, cum = decay_tables(step_ref[...], heads_ref)
    cum_s[...] = cum
    cumt_s[...] = cum.T
    dt_s[...] = dt
    same = segc_ref[...] == segr_ref[0]
    mask_ref[...] = jnp.where(same & (iota((n, n), 1) >= iota((n, n), 0)), 0.0, NEG)
    conv_ref[...] = jnp.zeros_like(conv_ref)
    head_ref[...] = jnp.zeros_like(head_ref)
    pairs = inner // LANES // parts
    base = part * pairs * LANES

    def at(main, tail, c0):
        return main[:, c0 - base : c0 - base + LANES] if c0 < inner else tail[:, c0 - inner : c0 - inner + LANES]

    def conv_back(c0, dv):
        x = at(xraw_m, xraw_t, c0).astype(F32)
        out = taps_ref[0:1, c0 : c0 + LANES] * dv
        conv_ref[0:1, c0 : c0 + LANES] += jnp.sum(dv * x, axis=0, keepdims=True)
        for k in range(1, taps):
            w = rows_of(dv * keep_ref[k - 1], -k, n)
            out = out + taps_ref[k : k + 1, c0 : c0 + LANES] * w
            conv_ref[k : k + 1, c0 : c0 + LANES] += jnp.sum(w * x, axis=0, keepdims=True)
        conv_ref[taps : taps + 1, c0 : c0 + LANES] += jnp.sum(dv, axis=0, keepdims=True)
        dx_ref[:, c0 - base : c0 - base + LANES] = out.astype(BF16)

    keys, queries = xact_t[:, :state], xact_t[:, state : 2 * state]
    gt_ref[...] = mm(keys, queries, 1, 1)
    for ref, k in ((dgt_ref, 0), (dcum_s, 1), (ddt_s, 2)):
        ref[...] = jnp.zeros_like(ref) if first else carried[k][...]
    left = iota((n, LANES), 1) < LANES // 2
    for p in range(part * pairs, (part + 1) * pairs):
        c0 = p * LANES
        here = slice(c0 - base, c0 - base + LANES)
        x = xact_m[:, here].astype(F32)
        dtp = pair_lanes(dt_s[...], p)
        xf = (x * dtp).astype(BF16).astype(F32)
        dy = dy_ref[:, here]
        dyf = dy.astype(F32)
        top, bottom = None, None
        for side in range(2):
            h = 2 * p + side
            lanes = left if side == 0 else ~left
            dys = jnp.where(lanes, dyf, 0.0).astype(BF16)
            xs = jnp.where(lanes, xf, 0.0).astype(BF16)
            e = jnp.exp((mask_ref[:t, :] + cumt_s[h : h + 1, :]) - cum_s[:t, h : h + 1])
            one = mm((gt_ref[:t, :] * e).astype(BF16), dys)
            dgt_ref[:t, :] += mm(xs[:t], dy, 1, 1) * e
            e = jnp.exp((mask_ref[t:, t:] + cumt_s[h : h + 1, t:]) - cum_s[t:, h : h + 1])
            two = mm((gt_ref[t:, t:] * e).astype(BF16), dys[t:])
            dgt_ref[t:, t:] += mm(xs[t:], dy[t:], 1, 1) * e
            top = one if top is None else top + one
            bottom = two if bottom is None else bottom + two
        dxt = jnp.concatenate([top, bottom], axis=0)
        skip = skip_ref[:, c0 : c0 + LANES]
        pick = jnp.where(iota((LANES, LANES), 0) // (LANES // 2) + 2 * p == iota((LANES, LANES), 1), 1.0, 0.0).astype(BF16)
        for ref, v in ((dcum_s, dyf * y_ref[:, here] - xf * dxt), (ddt_s, dxt * x)):
            hi = v.astype(BF16)
            ref[...] += mm(hi, pick) + mm((v - hi.astype(F32)).astype(BF16), pick)
        conv_ref[taps + 1 : taps + 2, c0 : c0 + LANES] += jnp.sum(dyf * x, axis=0, keepdims=True)
        conv_back(c0, (dxt * dtp + skip * dyf) * slope_m[:, here].astype(F32))
    if not last:
        return
    dgt = dgt_ref[...].astype(BF16)
    conv_back(inner, mm(dgt, queries) * slope_t[:, :state].astype(F32))
    conv_back(inner + state, mm(dgt, keys, 0, 0) * slope_t[:, state : 2 * state].astype(F32))
    later = jnp.where(iota((n, n), 1) >= iota((n, n), 0), 1.0, 0.0).astype(BF16)
    dld = exact_mm(later, dcum_s[...])
    dstep = (ddt_s[...] - rate * dld) * sigmoid(u)
    dx_ref[:, chan - base : chan - base + LANES] = dstep.astype(BF16)
    head_ref[0:1, :] += jnp.sum(dstep, axis=0, keepdims=True)
    head_ref[1:2, :] += jnp.sum(ld * dld, axis=0, keepdims=True)


def input_grad_kernel(hid_ref, cot_ref, gain_ref, dz_ref, da_ref, db_ref, za0, za1, a0, a1,
                      out_ref):
    half = za0.shape[0]
    dza, dxa, dxb = dz_ref[...], da_ref[...], db_ref[...]
    low = dxa.shape[1]
    f = hid_ref[...].astype(F32)
    inv = lax.rsqrt(jnp.mean(f * f, axis=1, keepdims=True) + EPSILON)

    total = jnp.zeros((f.shape[0], 1), F32)
    pieces = []
    for side, (p, q) in enumerate(((za0, a0), (za1, a1))):
        cols = slice(side * half, (side + 1) * half)
        dn = mm(dza, p[...], 1, 1) + mm(dxa, q[:, :low], 1, 1) + mm(dxb, q[:, low:], 1, 1)
        fs = f[:, cols]
        a = dn * gain_ref[:, cols]
        total = total + jnp.sum(a * fs, axis=1, keepdims=True)
        pieces.append(a)
    scale = total * (inv * inv * inv) / f.shape[1]
    for side, a in enumerate(pieces):
        cols = slice(side * half, (side + 1) * half)
        out_ref[:, cols] = (cot_ref[:, cols].astype(F32) + a * inv - f[:, cols] * scale).astype(BF16)


def call(kernel, args, in_specs, outs, out_specs, scratch, grid, flops, aliases={}):
    size = sum(a.size * a.dtype.itemsize for a in args) + sum(a.size * a.dtype.itemsize for a in outs)
    return pl.pallas_call(
        kernel,
        grid_spec=pltpu.PrefetchScalarGridSpec(
            num_scalar_prefetch=0, grid=grid, in_specs=in_specs, out_specs=out_specs, scratch_shapes=scratch
        ),
        out_shape=outs,
        cost_estimate=pl.CostEstimate(flops=flops, transcendentals=0, bytes_accessed=size),
        compiler_params=pltpu.CompilerParams(vmem_limit_bytes=60 * 1024 * 1024),
        input_output_aliases=aliases,
    )(*args)


def on_device(hidden_in, segment_ids, norm_gain, in_weight, conv_weight, conv_bias, gate_gain, out_weight,
              step_bias, decay_log, skip_weight, cotangent):
    count = lax.psum(1, AXES)
    bits, _ = plan(count)
    me = lax.axis_index(AXES)
    length, width = hidden_in.shape[1:]
    drow = in_weight.shape[0]
    erow = out_weight.shape[0]
    inner = erow * count
    taps = conv_weight.shape[0]
    xbc = conv_bias.shape[0] * count
    state = (xbc - inner) // 2
    heads = step_bias.shape[0]
    n = length // 2
    blocks = length // n
    pad = LANES - heads

    half = width // 2
    near = (2, 2) + (2,) * (bits - 3)
    wide = xbc + LANES
    cut = wide // 2 // LANES * LANES
    crow = conv_bias.shape[0]
    spare = drow >= 8 and max(crow, erow, drow) <= pad
    line = lambda v: jnp.pad(v.reshape(-1, v.shape[-1]), ((0, 0), (0, pad - v.shape[-1])))
    vectors = jnp.concatenate([line(v) for v in (conv_weight, conv_bias, gate_gain, norm_gain)])
    if spare:
        extra = jnp.pad(vectors, ((0, drow - vectors.shape[0]), (0, 0)))
    else:
        extra = jnp.zeros((drow, pad), BF16)
        small_rel = small_gather(vectors.reshape(1, -1), count).reshape(count, taps + 3, pad)
    first = jnp.concatenate([in_weight[:, inner:], extra], axis=1)
    f4 = far_gather(first, count)
    zc, oc = inner // 2, width // 2
    o = out_weight
    second = jnp.concatenate(
        [in_weight[:, :zc], o[:drow, :oc], o[drow:, :oc], in_weight[:, zc:inner], o[:drow, oc:], o[drow:, oc:]], axis=1)
    sc = zc + 2 * oc
    s4 = far_gather(second, count)
    fl, fr = near_gather(f4[..., :cut], f4[..., cut:], count)
    x0 = jnp.concatenate([fl, fr], axis=-1).reshape(half, wide)
    x1 = swap(x0, 1, count)
    sl, sr = near_gather(s4[..., :sc], s4[..., sc:], count)
    z0 = jnp.concatenate([sl[..., :zc], sr[..., :zc]], axis=-1).reshape(half, inner)
    w0 = jnp.concatenate([
        jnp.concatenate([v[..., zc : zc + oc], v[..., zc + oc :]], axis=-2) for v in (sl, sr)
    ], axis=-1).reshape(inner // 2, width)
    z1, w1 = swap(z0, 1, count), swap(w0, 1, count)

    spots = me ^ traced_bit_reverse(jnp.arange(count), bits)
    heads_in = jnp.pad(jnp.stack([step_bias, decay_log]), ((0, 6), (0, pad)))
    skip_in = jnp.repeat(skip_weight, inner // heads).reshape(1, inner)

    seg = segment_ids[0]
    n0 = jnp.sum((seg == 0).astype(jnp.int32))
    n1 = jnp.sum((seg == 1).astype(jnp.int32))
    shift = jnp.where(n1 == n, n0, 0)
    at = (jnp.arange(length) + shift) % length
    seg_rot = (at >= n0).astype(jnp.int32) + (at >= n0 + n1).astype(jnp.int32)
    turn = (at[:, None] == jnp.arange(length)[None, :]).astype(BF16)
    source = jnp.repeat(spots, drow) * drow + jnp.arange(width) % drow
    chans = (jnp.arange(width)[:, None] == source[None, :]).astype(BF16)
    exact = lambda a, b: jnp.dot(a, b, preferred_element_type=F32).astype(BF16)
    hid_r = exact(turn, hidden_in[0])
    cot_r = exact(turn, cotangent[0])
    hid_p = exact(hid_r, chans)
    cot_p = exact(cot_r, chans)
    me1 = me.reshape(1).astype(jnp.int32)
    smem = pl.BlockSpec(memory_space=pltpu.SMEM)
    if spare:
        edge = pl.BlockSpec((half, LANES), lambda i: (0, wide // LANES - 1))
        fixed = lambda r, c: pl.BlockSpec((r, c), lambda i: (0, 0))
        taps_in, gate_all, gain_rel = call(
            lambda *r: prep_kernel(*r, count=count, bits=bits, first=heads, sizes=(taps, crow, erow)),
            (me1, x0, x1), [smem, edge, edge],
            (jax.ShapeDtypeStruct((8, xbc), F32), jax.ShapeDtypeStruct((1, inner), F32), jax.ShapeDtypeStruct((1, width), F32)),
            (fixed(8, xbc), fixed(1, inner), fixed(1, width)),
            [pltpu.VMEM((8 * count, LANES), F32)], (1,), 2 * 8 * count * width * LANES,
        )
    else:
        own = ((me ^ jnp.arange(count))[None, :] == jnp.arange(count)[:, None]).astype(F32)
        small_all = jnp.einsum("dj,jrl->drl", own, small_rel.astype(F32), precision=lax.Precision.HIGHEST)
        vec = lambda r, size: small_all[:, r, :size].reshape(1, -1)
        gate_all = vec(taps + 1, erow)
        taps_in = jnp.pad(jnp.concatenate([vec(k, crow) for k in range(taps + 1)]), ((0, 8 - taps - 1), (0, 0)))
        gain_rel = exact(vec(taps + 2, drow).astype(BF16), chans).astype(F32)
    seg_b = seg_rot.reshape(blocks, n)
    lag = [jnp.pad(seg_b, ((0, 0), (k, 0)), constant_values=-1)[:, :n] == seg_b for k in range(taps)]
    cm = jnp.pad(jnp.stack(lag, axis=-1).astype(F32).reshape(length, taps), ((0, 0), (0, 8 - taps)))
    seg_col = seg_rot.reshape(length, 1)
    seg_row = seg_b.reshape(blocks, 1, n)

    rowblock = lambda c, b=None: pl.BlockSpec((n, c), (lambda i: (i, 0)) if b is None else (lambda i: (b, 0)))
    whole = lambda a: pl.BlockSpec(a.shape, lambda i: (0,) * a.ndim)
    segspec = lambda b: pl.BlockSpec((1, 1, n), lambda i: (b, 0, 0))
    anywhere = pl.BlockSpec(memory_space=pl.ANY)
    vm = lambda *s: pltpu.VMEM(s, F32)
    sds = jax.ShapeDtypeStruct
    square = 2 * n * n

    made = ()
    for b in range(blocks):
        args = (hid_p, gain_rel, x0, x1, taps_in, heads_in, cm, seg_col, seg_row)
        made = call(
            lambda *r: forward_kernel(*r, inner=inner, state=state, taps=taps),
            args + tuple(made),
            [rowblock(width, b)] + [whole(v) for v in args[1:6]] + [rowblock(8, b), rowblock(1, b), segspec(b)]
            + [anywhere] * len(made),
            (sds((length, width), BF16), sds((length, xbc), BF16), sds((length, LANES), F32),
             sds((length, xbc), BF16), sds((length, xbc), BF16), sds((length, inner), F32)),
            (rowblock(width, b), rowblock(xbc, b), rowblock(LANES, b), rowblock(xbc, b), rowblock(xbc, b), rowblock(inner, b)),
            [vm(n, wide), vm(taps - 1, n, LANES), vm(n, n), vm(n, n), vm(n, LANES), vm(LANES, n), vm(n, LANES)],
            (1,), 2 * n * width * wide + heads * square * LANES,
            {len(args) + k: k for k in range(len(made))},
        )
    normed, xraw, step, xact, slope, y = made

    move = erow % 16 == 0
    if not move:
        w0 = jnp.take(jnp.concatenate([w0, w1]).reshape(count, erow, width), traced_bit_reverse(me ^ jnp.arange(count), bits), axis=0)
        w0 = w0.reshape(inner, width)
        w1 = me1
    args = (me1, hid_r, cot_r, normed, y, xact, gate_all, skip_in, z0, z1, w0, w1)
    out_rot, gated, dy, dz, dgate = call(
        lambda *r: gate_kernel(*r, count=count, move=move),
        args,
        [smem, rowblock(width), rowblock(width), rowblock(width), rowblock(inner), rowblock(inner)]
        + [whole(v) for v in args[6:10]] + ([anywhere, anywhere] if move else [whole(w0), smem]),
        (sds((length, width), BF16), sds((length, inner), BF16), sds((length, inner), BF16),
         sds((length, inner), BF16), sds((8, inner), F32)),
        (rowblock(width), rowblock(inner), rowblock(inner), rowblock(inner), pl.BlockSpec((8, inner), lambda i: (0, 0))),
        [pltpu.VMEM((inner, width), BF16)] + [vm(n, inner)] * 4 + [pltpu.SemaphoreType.DMA((count,))],
        (blocks,), 3 * 2 * length * width * inner,
    )

    hrow = inner // 2
    if move:
        okeep, osend = call(
            lambda *r: out_grad_kernel(*r, count=count), (me1, gated, cot_r),
            [smem, whole(gated), whole(cot_r)], (sds((hrow, width), BF16),) * 2, (anywhere,) * 2,
            [pltpu.VMEM((inner, width), BF16), pltpu.SemaphoreType.DMA((count,))],
            (1,), 2 * length * width * inner,
        )
    else:
        gow = lax.dot_general(gated, cot_r, (((0,), (0,)), ((), ())), preferred_element_type=F32).astype(BF16)
        gow = jnp.take(gow.reshape(count, erow, width), spots, axis=0).reshape(inner, width)
        okeep, osend = gow[:hrow], gow[hrow:]

    def weight_grad(g, side):
        rows = normed[:, side * half : (side + 1) * half]
        return lax.dot_general(rows, g, (((0,), (0,)), ((), ())), preferred_element_type=F32).astype(BF16)

    zgot = swap(weight_grad(dz, 1), 1, count).reshape(near + (drow, inner))
    ogot = swap(osend, 1, count).reshape(near + (erow, width))
    zkeep = weight_grad(dz, 0).reshape(near + (drow, inner))
    okeep = okeep.reshape(near + (erow, width))

    def second_sum(c):
        def at_bits(i, j):
            zs = zkeep[i, j, ..., c * zc : (c + 1) * zc].astype(F32) + zgot[i, j, ..., c * zc : (c + 1) * zc].astype(F32)
            os = okeep[i, j, ..., c * oc : (c + 1) * oc].astype(F32) + ogot[i, j, ..., c * oc : (c + 1) * oc].astype(F32)
            return jnp.concatenate([zs, os[..., :drow, :], os[..., drow:, :]], axis=-1)

        return at_bits

    second_now = near_scatter(second_sum(0), second_sum(1), count)
    second_grad = far_scatter(second_now, count)

    parts = 2
    low = inner // parts
    made = [(), ()]
    sums = []
    for b in range(blocks):
        carry = ()
        for part in range(parts):
            cols = low if part == 0 else wide - low
            args = (xact, xact, slope, slope, xraw, xraw, y, dy, step, taps_in, heads_in, skip_in, cm, seg_col, seg_row)
            own = pl.BlockSpec((n, low), lambda i, b=b, part=part: (b, part))
            tail = pl.BlockSpec((n, 2 * state), lambda i, b=b: (b, inner // (2 * state)))
            fixed = lambda r, c: pl.BlockSpec((r, c), lambda i: (0, 0))
            dx, conv_sums, head_sums, *carry = call(
                lambda *r, part=part: backward_kernel(*r, inner=inner, state=state, taps=taps, part=part, parts=parts),
                args + made[part] + tuple(carry),
                [own, tail] * 3 + [own, own, rowblock(LANES, b)] + [whole(v) for v in args[9:12]]
                + [rowblock(8, b), rowblock(1, b), segspec(b)] + [anywhere] * len(made[part]) + [whole(v) for v in carry],
                (sds((length, cols), BF16), sds((8, wide), F32), sds((8, LANES), F32),
                 sds((n, n), F32), sds((n, LANES), F32), sds((n, LANES), F32)),
                (rowblock(cols, b), fixed(8, wide), fixed(8, LANES), fixed(n, n), fixed(n, LANES), fixed(n, LANES)),
                [vm(taps - 1, n, LANES), vm(n, n), vm(n, n), vm(n, LANES), vm(LANES, n), vm(n, LANES)],
                (1,), heads // parts * square * LANES * 2, {len(args): 0} if b else {},
            )
            made[part] = (dx,)
            sums.append((conv_sums, head_sums))
    dxa, dxb = made[0][0], made[1][0]
    conv_sums = sum(v[0] for v in sums[1:]) + sums[0][0]
    head_sums = sums[1][1] + sums[3][1]
    xsend = jnp.concatenate([weight_grad(dxa, 1), weight_grad(dxb, 1)], axis=1)
    xkeep = jnp.concatenate([weight_grad(dxa, 0), weight_grad(dxb, 0)], axis=1)
    xgot = swap(xsend, 1, count).reshape(near + (drow, wide))
    xkeep = xkeep.reshape(near + (drow, wide))

    def first_sum(lo, hi):
        return lambda i, j: xkeep[i, j, ..., lo:hi].astype(F32) + xgot[i, j, ..., lo:hi].astype(F32)

    first_now = near_scatter(first_sum(0, cut), first_sum(cut, wide), count)
    first_grad = far_scatter(first_now, count)

    args = (hid_p, cot_p, gain_rel, dz, dxa, dxb, z0, z1, x0, x1)
    hg = call(
        input_grad_kernel, args,
        [rowblock(width), rowblock(width), whole(gain_rel), rowblock(inner), rowblock(low), rowblock(wide - low)]
        + [whole(v) for v in args[6:]],
        (sds((length, width), BF16),), (rowblock(width),),
        [], (blocks,), 2 * length * width * (inner + wide),
    )[0]
    back = lambda v: lax.dot_general(turn, v, (((0,), (0,)), ((), ())), preferred_element_type=F32).astype(BF16)
    layer_out = back(out_rot)
    hidden_grad = back(lax.dot_general(hg, chans, (((1,), (1,)), ((), ())), preferred_element_type=F32).astype(BF16))

    skip_sum = conv_sums[taps + 1, :inner].reshape(heads, -1).sum(axis=1)
    flat = jnp.concatenate([
        dgate[0], conv_sums[: taps + 1, :xbc].reshape(-1), head_sums[0, :heads], head_sums[1, :heads], skip_sum,
    ])
    flat = jnp.pad(flat, (0, -flat.shape[0] % 1024)).reshape(-1, LANES)
    flat = sum_everywhere(flat, count).reshape(-1)
    o2 = inner + xbc * (taps + 1)
    mine = lambda v, size: lax.dynamic_slice_in_dim(v, me * size, size, axis=-1)
    conv_tot = mine(flat[inner:o2].reshape(taps + 1, xbc), xbc // count)
    grad_in_weight = jnp.concatenate(
        [second_grad[:, :zc], second_grad[:, sc : sc + zc], first_grad[:, : wide - pad]], axis=1)
    grad_norm_gain = jnp.sum(in_weight.astype(F32) * grad_in_weight, axis=1) / norm_gain.astype(F32)
    sg = second_grad
    return (
        layer_out[None],
        hidden_grad[None],
        grad_norm_gain,
        grad_in_weight,
        conv_tot[:taps],
        conv_tot[taps],
        mine(flat[:inner], erow),
        jnp.concatenate([
            jnp.concatenate([sg[:, c * sc + zc : c * sc + zc + oc], sg[:, c * sc + zc + oc : (c + 1) * sc]], axis=0)
            for c in range(2)
        ], axis=1),
        flat[o2 : o2 + heads],
        flat[o2 + heads : o2 + 2 * heads],
        flat[o2 + 2 * heads : o2 + 3 * heads],
    )


def solution(mesh):
    rows = P(AXES, None)
    placed = (
        P(AXES, None, None), rows, P(AXES), rows, P(None, AXES), P(AXES), P(AXES), rows,
        P(), P(), P(), P(AXES, None, None),
    )
    return jax.shard_map(
        on_device,
        mesh=mesh,
        in_specs=placed,
        out_specs=(
            P(AXES, None, None), P(AXES, None, None), P(AXES), rows, P(None, AXES), P(AXES), P(AXES), rows,
            P(), P(), P(),
        ),
        check_vma=False,
    )
```
